32 devices in a mesh: row: 4 (over y, core), col: 8 (over z, x).
Axes of the slice: x: 2, y: 2, z: 4, core: 2. Of those that a mesh axis runs over, the one named last changes fastest.
Arguments:
- inverse: float32 [16384, 16384], P('row', 'col'), may hold values from -6 to 6
- front_blocks: int32 [2, 16], replicated, may hold values from 0 to 63, as said below
- panels: float32 [2, 4096, 256], P(None, 'row'), may hold values from -0.09375 to 0.09375
- diag_terms: float32 [2, 256, 256], replicated, may hold values from -6 to 6
- bounds: int32 [2, 4], replicated, may hold values from 1 to 128, 256 in all within a row
Outputs:
- border: float32 [2, 4096, 256], P(None, ('row', 'col'))
- diag_block: float32 [2, 256, 256], replicated
The draws below stay inside these ranges and needn't reach their ends.
Inputs may be any that keep to these rules, and one draw needn't show every extreme that they name: `front_blocks`: each row names 16 distinct blocks. Positions 4 r to 4 r + 3 name blocks of four different groups of 16 consecutive blocks, and every such group is named at exactly four positions, of four different r. Positions 2 o and 2 o + 1 name blocks of two different groups of 8 consecutive blocks, and every such group is named at exactly two positions, of two different o.
All inputs are finite; a program needn't handle non-finite values.
Results may differ from the reference program's by a relative error of at most 0.0001.
Values sent between devices are 32-bit elements; how exact they have to be, the bound alone decides.
A program may use at most 128 MiB of HBM per device.

```python
import math
import jax
import jax.numpy as jnp
import numpy as np
from jax import lax

ORDER = 16384
BS = 256
PC = 256
NSUP = 4
FRONTS = 2
KB = 16
MF = 4096
N_ROW = 4
N_COL = 8


def draw_front_blocks(key, part):
    block_count = ORDER // BS
    group_size = block_count // N_COL
    chosen_rows = []
    for front_index in range(2):
        front_key = jax.random.fold_in(key, 101 + front_index)
        subkeys = jax.random.split(front_key, 4)
        order_rows = jax.random.permutation(subkeys[0], N_ROW)
        offset = jax.random.randint(subkeys[1], (), 0, N_ROW)
        flip_bits = jax.random.randint(subkeys[2], (N_ROW,), 0, 2)
        within = jax.vmap(lambda subkey: jax.random.permutation(subkey, group_size))(jax.random.split(subkeys[3], N_COL))
        position = jnp.arange(KB)
        holder = position // 2
        second = position % 2
        row_holder = holder // 2
        shift_step = 2 * (holder % 2) + second
        region = order_rows[(row_holder + offset + shift_step) % N_ROW]
        column_group = 2 * region + (second + flip_bits[region]) % 2
        chosen = column_group * group_size + within[column_group, holder % 2]
        chosen_rows.append(chosen)
    return jnp.stack(chosen_rows).astype(jnp.int32)


def steps_of(key, shape, cuts, low, largest):
    def one(axis_at, blocks):
        heights = jax.random.uniform(jax.random.fold_in(jax.random.fold_in(key, 6), axis_at), (blocks,), jnp.float32, low / len(cuts), largest / len(cuts))
        return jnp.repeat(jnp.exp(heights), shape[axis_at] // blocks).reshape((-1,) + (1,) * (len(shape) - axis_at - 1))

    gain = one(*cuts[0])
    for cut in cuts[1:]:
        gain = gain * one(*cut)
    return gain


def profile(count, total, reach, slope):
    loads = [(1 << 20) // math.isqrt(standing ** slope) + 1 for standing in range(2, count + 1)]
    spare, holding = total - reach - (count - 1), [1] * (count - 1)
    while spare > 0:
        movable = [i for i in range(count - 1) if holding[i] < reach]
        mass, left = sum([loads[i] for i in movable]), spare
        for i in movable:
            extra = min(reach - holding[i], max(1, left * loads[i] // mass), spare)
            holding[i] = holding[i] + extra
            spare = spare - extra
    return np.array([reach] + holding)


def uneven(key, amount, total, most, skew):
    if amount == 2:
        one = jax.random.randint(key, (), max(1, total - most), min(most, total - 1) + 1)
        return jnp.stack([one, total - one])
    sizes = jnp.asarray(profile(amount, total, most, skew), jnp.int32)
    twos = (amount - 1) // 2
    donor, taker = sizes[1:1 + 2 * twos:2], sizes[2:2 + 2 * twos:2]
    margin = jnp.minimum(donor - 1, most - taker)
    passed = jax.random.randint(jax.random.fold_in(key, 1), (twos,), 0, 1 << 20) % (margin + 1)
    sizes = sizes.at[1:1 + 2 * twos:2].set(donor - passed).at[2:2 + 2 * twos:2].set(taker + passed)
    return sizes[jax.random.permutation(jax.random.fold_in(key, 2), amount)]


def centred(rng, extent, spread, bound, shards=(), held_as=jnp.bfloat16):
    values = jax.random.normal(rng, extent, jnp.float32) * spread
    if len(shards) > 0:
        values = steps_of(rng, extent, shards, -0.22, 0.18) * values
    return jnp.clip(values, min=-bound, max=bound).astype(held_as)


def setup_inputs(seed: int = 0) -> dict:
    key_of = jax.random.split(jax.random.key(seed), 6)
    return {
        "inverse": centred(key_of[0], (ORDER, ORDER), 1.0, 6.0, ((0, 4), (1, 8)), jnp.float32),
        "front_blocks": draw_front_blocks(jax.random.fold_in(key_of[5], 71), 0),
        "panels": centred(key_of[2], (FRONTS, MF, PC), MF ** -0.5, 0.09375, ((1, 4),), jnp.float32),
        "diag_terms": centred(key_of[3], (FRONTS, PC, PC), 1.0, 6.0, (), jnp.float32),
        "bounds": jax.vmap(lambda own: uneven(own, NSUP, PC, PC // 2, 2))(jax.random.split(key_of[4], FRONTS)).reshape((FRONTS, NSUP)).astype(jnp.int32),
    }


def reference(inverse, front_blocks, panels, diag_terms, bounds):
    block_count = ORDER // BS
    tile_grid = inverse.reshape(block_count, BS, block_count, BS)
    borders = []
    diagonals = []
    for front_index in range(2):
        front_list = front_blocks[front_index].astype(jnp.int32)
        front_inverse = jnp.take(tile_grid, front_list, axis=0)
        front_inverse = jnp.take(front_inverse, front_list, axis=2).reshape(MF, MF)
        border = -jnp.dot(front_inverse, panels[front_index], precision=lax.Precision.HIGHEST)
        node_ends = jnp.cumsum(bounds[front_index])
        columns = jnp.arange(PC, dtype=jnp.int32)
        node_ids = jnp.sum((columns[:, None] >= node_ends[None, :]).astype(jnp.int32), axis=1)
        same_node = (node_ids[:, None] == node_ids[None, :]).astype(jnp.float32)
        inner = jnp.dot(panels[front_index].T, border, precision=lax.Precision.HIGHEST)
        borders.append(border)
        diagonals.append(same_node * (diag_terms[front_index] - inner))
    return (jnp.stack(borders), jnp.stack(diagonals))
```

```python
import functools

import jax
import jax.numpy as jnp
from jax import lax
from jax.experimental import pallas as pl
from jax.experimental.pallas import tpu as pltpu
from jax.sharding import PartitionSpec as P

BS = 256


def split(a):
    hi = a.astype(jnp.bfloat16)
    lo = (a - hi.astype(jnp.float32)).astype(jnp.bfloat16)
    return hi, lo


def dot3(a, b):
    ah, al = a
    bh, bl = b
    dot = functools.partial(jnp.dot, preferred_element_type=jnp.float32)
    return dot(ah, bh) + (dot(ah, bl) + dot(al, bh))


def tile_kernel(dims, fb, inv, w, out, tiles, sem):
    fronts, kb, nr, nc, rg, cg, nz, nx = dims
    r = lax.axis_index("row")
    c = lax.axis_index("col")
    per_owner = kb // lax.axis_size("row")
    owners = []
    for f in range(fronts):
        rows = [jnp.int32(0)] * nr
        cols = [jnp.int32(0)] * nc
        own = [jnp.int32(0)] * nc
        n = jnp.int32(0)
        m = jnp.int32(0)
        for p in range(kb):
            b = fb[f, p]
            here = (b // rg) == r
            for i in range(nr):
                rows[i] = jnp.where(here & (n == i), b % rg, rows[i])
            n = n + here.astype(jnp.int32)
            there = (b // cg) == c
            for i in range(nc):
                hit = there & (m == i)
                cols[i] = jnp.where(hit, b % cg, cols[i])
                own[i] = jnp.where(hit, p // per_owner, own[i])
            m = m + there.astype(jnp.int32)
        owners.append(own)
        for k in range(nc):
            for i in range(nr):
                pltpu.make_async_copy(
                    inv.at[
                        pl.ds(pl.multiple_of(rows[i] * BS, BS), BS),
                        pl.ds(pl.multiple_of(cols[k] * BS, BS), BS),
                    ],
                    tiles.at[f, k, pl.ds(i * BS, BS)],
                    sem.at[f, k, i],
                ).start()
    sub = BS // (nz * nx)
    for f in range(fronts):
        total = None
        for k in range(nc):
            for i in range(nr):
                pltpu.make_async_copy(
                    inv.at[pl.ds(0, BS), pl.ds(0, BS)],
                    tiles.at[f, k, pl.ds(i * BS, BS)],
                    sem.at[f, k, i],
                ).wait()
            term = dot3(split(tiles[f, k]), split(w[owners[f][k], f]))
            total = term if total is None else total + term
        for i in range(nr):
            for s in range(nx):
                for z in range(nz):
                    at = i * BS + (s * nz + z) * sub
                    out[z * nx + s, f, i] = total[at : at + sub]


def body(inverse, front_blocks, panels, diag_terms, bounds):
    n_row = lax.axis_size("row")
    n_col = lax.axis_size("col")
    r = lax.axis_index("row")
    c = lax.axis_index("col")
    rows_loc, cols_loc = inverse.shape
    rg = rows_loc // BS
    cg = cols_loc // BS
    fronts, kb = front_blocks.shape
    width = panels.shape[2]
    per_owner = kb // n_row
    nr = kb // n_row
    nc = kb // n_col
    nz = per_owner
    nx = n_col // nz
    sub = BS // n_col
    share = nz * sub

    owner_rows = front_blocks.reshape(fronts, n_row, per_owner)
    mine = lax.dynamic_index_in_dim(owner_rows, r, 1, keepdims=False)
    pick = (mine // cg) == c
    pieces = panels.reshape(fronts, per_owner, BS, width)
    own_piece = jnp.sum(jnp.where(pick[:, :, None, None], pieces, 0.0), axis=1)
    gathered = lax.all_gather(own_piece, "row", axis=0, tiled=False)

    dims = (fronts, kb, nr, nc, rg, cg, nz, nx)
    partial = pl.pallas_call(
        functools.partial(tile_kernel, dims),
        out_shape=jax.ShapeDtypeStruct((n_col, fronts, nr, sub, width), jnp.float32),
        in_specs=[
            pl.BlockSpec(memory_space=pltpu.SMEM),
            pl.BlockSpec(memory_space=pl.ANY),
            pl.BlockSpec(memory_space=pltpu.VMEM),
        ],
        out_specs=pl.BlockSpec(memory_space=pltpu.VMEM),
        scratch_shapes=[
            pltpu.VMEM((fronts, nc, nr * BS, BS), jnp.float32),
            pltpu.SemaphoreType.DMA((fronts, nc, nr)),
        ],
        compiler_params=pltpu.CompilerParams(vmem_limit_bytes=40 << 20),
    )(front_blocks, inverse, gathered)

    reduced = lax.psum_scatter(partial, "col", scatter_dimension=0, tiled=False)
    groups = front_blocks // rg
    if nr == n_row:
        slots = jnp.swapaxes(reduced, 0, 1)
    else:
        named = jnp.any((groups == r).reshape(fronts, n_row, per_owner), axis=-1)
        place = jnp.cumsum(named.astype(jnp.int32), axis=1) - 1
        chosen = named[:, :, None] & (place[:, :, None] == jnp.arange(nr))
        slots = jnp.sum(
            jnp.where(chosen.transpose(1, 0, 2)[..., None, None], reduced[None], 0.0), axis=2
        )
    received = lax.all_to_all(slots, "row", split_axis=0, concat_axis=0, tiled=True)
    sources = lax.dynamic_index_in_dim(
        groups.reshape(fronts, n_row, per_owner), r, 1, keepdims=False
    )
    chosen = sources.T[:, None, :] == jnp.arange(n_row, dtype=jnp.int32)[None, :, None]
    ordered = jnp.sum(jnp.where(chosen[..., None, None], received[None], 0.0), axis=1)
    lines = [[z * nx + s for z in range(nz)] for s in range(nx)]
    product = lax.all_to_all(
        ordered, "col", split_axis=0, concat_axis=0, axis_index_groups=lines, tiled=True
    )
    product = jnp.swapaxes(product, 0, 1).reshape(fronts, share, width)
    w_mine = lax.dynamic_slice_in_dim(panels, c * share, share, 1)
    own_term = jnp.einsum(
        "fsa,fsb->fab", w_mine, product, precision=lax.Precision.HIGHEST
    )
    summed = lax.psum(own_term, ("row", "col"))
    ends = jnp.cumsum(bounds, axis=1)
    columns = jnp.arange(width, dtype=jnp.int32)
    ids = jnp.sum((columns[None, :, None] >= ends[:, None, :]).astype(jnp.int32), axis=2)
    same = (ids[:, :, None] == ids[:, None, :]).astype(jnp.float32)
    return (-product, same * (diag_terms + summed))


def solution(mesh):
    placed = (P("row", "col"), P(), P(None, "row", None), P(), P())
    return jax.shard_map(
        body,
        mesh=mesh,
        in_specs=placed,
        out_specs=(P(None, ("row", "col"), None), P()),
        check_vma=False,
    )
```

```python
import functools

import jax
import jax.numpy as jnp
from jax import lax
from jax.experimental import pallas as pl
from jax.experimental.pallas import tpu as pltpu
from jax.sharding import PartitionSpec as P

BS = 256


def split(a):
    hi = a.astype(jnp.bfloat16)
    lo = (a - hi.astype(jnp.float32)).astype(jnp.bfloat16)
    return hi, lo


def dot3(a, b):
    ah, al = a
    bh, bl = b
    dot = functools.partial(jnp.dot, preferred_element_type=jnp.float32)
    return dot(ah, bh) + (dot(ah, bl) + dot(al, bh))


def tile_kernel(dims, fb, inv, w, out, tiles, sem):
    fronts, kb, nr, nc, rg, cg, nz, nx = dims
    r = lax.axis_index("row")
    c = lax.axis_index("col")
    per_owner = kb // lax.axis_size("row")
    owners = []
    for f in range(fronts):
        rows = [jnp.int32(0)] * nr
        cols = [jnp.int32(0)] * nc
        own = [jnp.int32(0)] * nc
        n = jnp.int32(0)
        m = jnp.int32(0)
        for p in range(kb):
            b = fb[f, p]
            here = (b // rg) == r
            for i in range(nr):
                rows[i] = jnp.where(here & (n == i), b % rg, rows[i])
            n = n + here.astype(jnp.int32)
            there = (b // cg) == c
            for i in range(nc):
                hit = there & (m == i)
                cols[i] = jnp.where(hit, b % cg, cols[i])
                own[i] = jnp.where(hit, p // per_owner, own[i])
            m = m + there.astype(jnp.int32)
        owners.append(own)
        for k in range(nc):
            for i in range(nr):
                pltpu.make_async_copy(
                    inv.at[
                        pl.ds(pl.multiple_of(rows[i] * BS, BS), BS),
                        pl.ds(pl.multiple_of(cols[k] * BS, BS), BS),
                    ],
                    tiles.at[f, k, pl.ds(i * BS, BS)],
                    sem.at[f, k, i],
                ).start()
    sub = BS // (nz * nx)
    for f in range(fronts):
        total = None
        for k in range(nc):
            for i in range(nr):
                pltpu.make_async_copy(
                    inv.at[pl.ds(0, BS), pl.ds(0, BS)],
                    tiles.at[f, k, pl.ds(i * BS, BS)],
                    sem.at[f, k, i],
                ).wait()
            term = dot3(split(tiles[f, k]), split(w[owners[f][k], f]))
            total = term if total is None else total + term
        for i in range(nr):
            for s in range(nx):
                for z in range(nz):
                    at = i * BS + (s * nz + z) * sub
                    out[f, s, i, z] = total[at : at + sub]


MESH = pl.DeviceIdType.MESH


def greet(peers):
    barrier = pltpu.get_barrier_semaphore()
    for peer in peers:
        pl.semaphore_signal(barrier, inc=1, device_id=peer, device_id_type=MESH)
    pl.semaphore_wait(barrier, len(peers))


class Mail:
    def __init__(self, send_sem, recv_sem):
        self.send_sem, self.recv_sem = send_sem, recv_sem
        self.sent = []

    def send(self, src, dst, peer):
        at = len(self.sent)
        copy = pltpu.make_async_remote_copy(
            src_ref=src,
            dst_ref=dst,
            send_sem=self.send_sem.at[at],
            recv_sem=self.recv_sem.at[at],
            device_id=peer,
            device_id_type=MESH,
        )
        copy.start()
        self.sent.append(copy)
        return copy

    def close(self):
        for copy in self.sent:
            copy.wait_send()


def gather_kernel(dims, fb, panels, out, send_sem, recv_sem):
    fronts, n_row, cg, cuts = dims
    r = lax.axis_index("row")
    c = lax.axis_index("col")
    core, y, ny = lax.rem(r, 2), r // 2, n_row // 2
    partner = r + 1 - 2 * core
    lines = [lax.rem(y + d, ny) * 2 + core for d in range(1, ny)]
    greet([(partner, c)] + [(line, c) for line in lines])
    per_owner = panels.shape[1]
    mail = Mail(send_sem, recv_sem)
    height = BS // cuts
    arriving, relayed = [], []
    for f in range(fronts):
        at = jnp.int32(0)
        found = jnp.int32(0)
        for j in range(per_owner):
            hit = (fb[f, r * per_owner + j] // cg) == c
            at = jnp.where(hit, j, at)
            found = jnp.where(hit, 1, found)
        out[r, f] = jnp.where(found == 1, panels[f, at], 0.0)
        for h in range(cuts):
            rows = pl.ds(h * height, height)
            for d, line in enumerate(lines, 1):
                piece = out.at[r, f, rows]
                came = lax.rem(y + ny - d, ny) * 2 + core
                arriving.append((mail.send(piece, piece, (line, c)), came, f, rows))
        mine = out.at[r, f]
        relayed.append(mail.send(mine, mine, (partner, c)))
    for copy, came, f, rows in arriving:
        copy.wait_recv()
        piece = out.at[came, f, rows]
        relayed.append(mail.send(piece, piece, (partner, c)))
    for copy in relayed:
        copy.wait_recv()
    mail.close()


def copies_of(dims):
    fronts, kb, nr, nc, rg, cg, nz, nx = dims
    n_row, n_col = kb // nr, kb // nc
    total = nr * (nx - 1) + nr * (nz - 1) + (n_row - 1) + (nz - 1)
    return fronts * (total + 2 * (1 + n_row // 2 - 1 + n_col - 1))


def sum_kernel(dims, fb, partial, w, border, acc, xbuf, xs, zbuf, zs, slots, rbuf, qs, cbuf, ybuf, lbuf, red, send_sem, recv_sem):
    fronts, kb, nr, nc, rg, cg, nz, nx = dims
    n_row, n_col = kb // nr, kb // nc
    per_owner = kb // n_row
    r = lax.axis_index("row")
    c = lax.axis_index("col")
    s, z = lax.rem(c, nx), c // nx
    core, y, ny = lax.rem(r, 2), r // 2, n_row // 2
    partner = r + 1 - 2 * core
    other = 1 - core
    cols = [lax.rem(c + d, n_col) for d in range(1, n_col)]
    rows = [lax.rem(r + d, n_row) for d in range(1, n_row)]
    greet([(r, col) for col in cols] + [(row, c) for row in rows])
    mail = Mail(send_sem, recv_sem)
    width = w.shape[2]
    share = w.shape[1]
    part = acc.shape[4]
    sub = zs.shape[2]

    along_x = {}
    for f in range(fronts):
        for n in range(nr):
            for d in range(1, nx):
                to = lax.rem(s + d, nx)
                along_x[f, n, d] = mail.send(
                    partial.at[f, to, n], xbuf.at[f, n, d - 1], (r, z * nx + to)
                )

    along_z = {}

    def x_sum(f, n):
        for d in range(1, nx):
            along_x[f, n, d].wait_recv()
        total = partial[f, s, n]
        for d in range(1, nx):
            total = total + xbuf[f, n, d - 1]
        xs[f, n] = total
        for d in range(1, nz):
            to = lax.rem(z + d, nz)
            along_z[f, n, d] = mail.send(
                xs.at[f, n, to], zbuf.at[f, n, d - 1], (r, to * nx + s)
            )

    def z_sum(f, n):
        for d in range(1, nz):
            along_z[f, n, d].wait_recv()
        total = xs[f, n, z]
        for d in range(1, nz):
            total = total + zbuf[f, n, d - 1]
        zs[f, n] = total

    along_row = {}

    def row_send(f):
        if nr == n_row:
            source = zs
        else:
            source = slots
            n = jnp.int32(0)
            for row in range(n_row):
                named = jnp.int32(0)
                for j in range(per_owner):
                    named = jnp.where((fb[f, row * per_owner + j] // rg) == r, 1, named)
                slots[f, row] = jnp.where(named == 1, zs[f, jnp.minimum(n, nr - 1)], 0.0)
                n = n + named
        rbuf[f][r] = source[f, r]
        for d in range(1, n_row):
            to = rows[d - 1]
            along_row[f, d] = mail.send(source.at[f, to], rbuf[f].at[r], (to, c))

    along_owner = {}

    def owner_send(f):
        for d in range(1, n_row):
            along_row[f, d].wait_recv()
        for q in range(nz):
            qs[f, q] = rbuf[f][fb[f, r * per_owner + q] // rg]
        border[f, z] = qs[f, z]
        for d in range(1, nz):
            to = lax.rem(z + d, nz)
            along_owner[f, d] = mail.send(qs.at[f, to], border.at[f, z], (r, to * nx + s))

    to_core = {}

    def product(f):
        for d in range(1, nz):
            along_owner[f, d].wait_recv()
        wh, wl = split(w[f])
        ph, plo = split(jnp.concatenate([border[f, q] for q in range(nz)], axis=0))
        dot = functools.partial(
            lax.dot_general,
            dimension_numbers=(((0,), (0,)), ((), ())),
            preferred_element_type=jnp.float32,
        )
        total = dot(wh, ph) + (dot(wh, plo) + dot(wl, ph))
        for a in range(2):
            for b in range(ny):
                for e in range(n_col):
                    at = ((a * ny + b) * n_col + e) * part
                    red[f, a, b, e] = total[at : at + part]
        to_core[f] = mail.send(red.at[f, other], cbuf.at[f], (partner, c))

    to_y = {}

    def core_sum(f):
        to_core[f].wait_recv()
        red[f, core] = red[f, core] + cbuf[f]
        for d in range(1, ny):
            to = lax.rem(y + d, ny)
            to_y[f, d] = mail.send(
                red.at[f, core, to], ybuf.at[f, d - 1], (to * 2 + core, c)
            )

    to_col = {}

    def y_sum(f):
        for d in range(1, ny):
            to_y[f, d].wait_recv()
        total = red[f, core, y]
        for d in range(1, ny):
            total = total + ybuf[f, d - 1]
        red[f, core, y] = total
        for d in range(1, n_col):
            to = cols[d - 1]
            to_col[f, d] = mail.send(red.at[f, core, y, to], lbuf.at[f, d - 1], (r, to))

    back_col = {}

    def col_sum(f):
        for d in range(1, n_col):
            to_col[f, d].wait_recv()
        total = red[f, core, y, c]
        for d in range(1, n_col):
            total = total + lbuf[f, d - 1]
        acc[f, core, y, c] = total
        mine = acc.at[f, core, y, c]
        for d in range(1, n_col):
            back_col[f, d] = mail.send(mine, mine, (r, cols[d - 1]))

    back_y = {}

    def y_back(f):
        for d in range(1, n_col):
            back_col[f, d].wait_recv()
        mine = acc.at[f, core, y]
        for d in range(1, ny):
            to = lax.rem(y + d, ny)
            back_y[f, d] = mail.send(mine, mine, (to * 2 + core, c))

    back_core = {}

    def core_back(f):
        for d in range(1, ny):
            back_y[f, d].wait_recv()
        mine = acc.at[f, core]
        back_core[f] = mail.send(mine, mine, (partner, c))

    def finish(f):
        back_core[f].wait_recv()

    for n in range(nr):
        x_sum(0, n)
    for f in range(fronts):
        for n in range(nr):
            if f + 1 < fronts:
                x_sum(f + 1, n)
            z_sum(f, n)
            if f > 0 and n == nr // 2 - 1:
                owner_send(f - 1)
        row_send(f)
        if f > 0:
            product(f - 1)
    last = fronts - 1
    owner_send(last)
    for f in range(last):
        core_sum(f)
    product(last)
    for f in range(last):
        y_sum(f)
    core_sum(last)
    for f in range(last):
        col_sum(f)
    y_sum(last)
    for f in range(last):
        y_back(f)
    col_sum(last)
    for f in range(last):
        core_back(f)
    y_back(last)
    core_back(last)
    for f in range(fronts):
        finish(f)
    mail.close()


def body(inverse, front_blocks, panels, diag_terms, bounds):
    n_row = lax.axis_size("row")
    n_col = lax.axis_size("col")
    r = lax.axis_index("row")
    c = lax.axis_index("col")
    rows_loc, cols_loc = inverse.shape
    rg = rows_loc // BS
    cg = cols_loc // BS
    fronts, kb = front_blocks.shape
    width = panels.shape[2]
    per_owner = kb // n_row
    nr = kb // n_row
    nc = kb // n_col
    nz = per_owner
    nx = n_col // nz
    sub = BS // n_col
    share = nz * sub

    cuts = 2
    gdims = (fronts, n_row, cg, cuts)
    count = fronts * (cuts * 2 * (n_row // 2 - 1) + 1)
    vmem = pl.BlockSpec(memory_space=pltpu.VMEM)
    smem = pl.BlockSpec(memory_space=pltpu.SMEM)
    gathered = pl.pallas_call(
        functools.partial(gather_kernel, gdims),
        out_shape=jax.ShapeDtypeStruct((n_row, fronts, BS, width), jnp.float32),
        in_specs=[smem, vmem],
        out_specs=vmem,
        scratch_shapes=[pltpu.SemaphoreType.DMA((count,))] * 2,
        compiler_params=pltpu.CompilerParams(
            collective_id=0, has_side_effects=True, vmem_limit_bytes=24 << 20
        ),
    )(front_blocks, panels.reshape(fronts, per_owner, BS, width))

    dims = (fronts, kb, nr, nc, rg, cg, nz, nx)
    partial = pl.pallas_call(
        functools.partial(tile_kernel, dims),
        out_shape=jax.ShapeDtypeStruct((fronts, nx, nr, nz, sub, width), jnp.float32),
        in_specs=[
            pl.BlockSpec(memory_space=pltpu.SMEM),
            pl.BlockSpec(memory_space=pl.ANY),
            pl.BlockSpec(memory_space=pltpu.VMEM),
        ],
        out_specs=pl.BlockSpec(memory_space=pltpu.VMEM),
        scratch_shapes=[
            pltpu.VMEM((fronts, nc, nr * BS, BS), jnp.float32),
            pltpu.SemaphoreType.DMA((fronts, nc, nr)),
        ],
        compiler_params=pltpu.CompilerParams(vmem_limit_bytes=40 << 20),
    )(front_blocks, inverse, gathered)

    w_mine = lax.dynamic_slice_in_dim(panels, c * share, share, 1)
    ny = n_row // 2
    part = width // (n_row * n_col)
    count = copies_of(dims)
    f32 = jnp.float32
    border, acc = pl.pallas_call(
        functools.partial(sum_kernel, dims),
        out_shape=(
            jax.ShapeDtypeStruct((fronts, nz, sub, width), f32),
            jax.ShapeDtypeStruct((fronts, 2, ny, n_col, part, width), f32),
        ),
        in_specs=[smem, vmem, vmem],
        out_specs=(vmem, vmem),
        scratch_shapes=[
            pltpu.VMEM((fronts, nr, nx - 1, nz, sub, width), f32),
            pltpu.VMEM((fronts, nr, nz, sub, width), f32),
            pltpu.VMEM((fronts, nr, nz - 1, sub, width), f32),
            pltpu.VMEM((fronts, nr, sub, width), f32),
            pltpu.VMEM((fronts, n_row, sub, width), f32),
            [pltpu.VMEM((n_row, sub, width), f32)] * fronts,
            pltpu.VMEM((fronts, nz, sub, width), f32),
            pltpu.VMEM((fronts, ny, n_col, part, width), f32),
            pltpu.VMEM((fronts, ny - 1, n_col, part, width), f32),
            pltpu.VMEM((fronts, n_col - 1, part, width), f32),
            pltpu.VMEM((fronts, 2, ny, n_col, part, width), f32),
            pltpu.SemaphoreType.DMA((count,)),
            pltpu.SemaphoreType.DMA((count,)),
        ],
        compiler_params=pltpu.CompilerParams(
            collective_id=1, has_side_effects=True, vmem_limit_bytes=40 << 20
        ),
    )(front_blocks, partial, w_mine)
    product = border.reshape(fronts, share, width)
    summed = acc.reshape(fronts, width, width)
    ends = jnp.cumsum(bounds, axis=1)
    columns = jnp.arange(width, dtype=jnp.int32)
    ids = jnp.sum((columns[None, :, None] >= ends[:, None, :]).astype(jnp.int32), axis=2)
    same = (ids[:, :, None] == ids[:, None, :]).astype(jnp.float32)
    return (-product, same * (diag_terms + summed))


def solution(mesh):
    placed = (P("row", "col"), P(), P(None, "row", None), P(), P())
    return jax.shard_map(
        body,
        mesh=mesh,
        in_specs=placed,
        out_specs=(P(None, ("row", "col"), None), P()),
        check_vma=False,
    )
```

```python
import functools

import jax
import jax.numpy as jnp
from jax import lax
from jax.experimental import pallas as pl
from jax.experimental.pallas import tpu as pltpu
from jax.sharding import PartitionSpec as P

BS = 256


def split(a):
    hi = a.astype(jnp.bfloat16)
    lo = (a - hi.astype(jnp.float32)).astype(jnp.bfloat16)
    return hi, lo


def dot3(a, b):
    ah, al = a
    bh, bl = b
    dot = functools.partial(jnp.dot, preferred_element_type=jnp.float32)
    return dot(ah, bh) + (dot(ah, bl) + dot(al, bh))


def tile_kernel(dims, fb, inv, w, out, tiles, sem):
    fronts, kb, nr, nc, rg, cg, nz, nx = dims
    r = lax.axis_index("row")
    c = lax.axis_index("col")
    per_owner = kb // lax.axis_size("row")
    owners = []
    for f in range(fronts):
        rows = [jnp.int32(0)] * nr
        cols = [jnp.int32(0)] * nc
        own = [jnp.int32(0)] * nc
        n = jnp.int32(0)
        m = jnp.int32(0)
        for p in range(kb):
            b = fb[f, p]
            here = (b // rg) == r
            for i in range(nr):
                rows[i] = jnp.where(here & (n == i), b % rg, rows[i])
            n = n + here.astype(jnp.int32)
            there = (b // cg) == c
            for i in range(nc):
                hit = there & (m == i)
                cols[i] = jnp.where(hit, b % cg, cols[i])
                own[i] = jnp.where(hit, p // per_owner, own[i])
            m = m + there.astype(jnp.int32)
        owners.append(own)
        for k in range(nc):
            for i in range(nr):
                pltpu.make_async_copy(
                    inv.at[
                        pl.ds(pl.multiple_of(rows[i] * BS, BS), BS),
                        pl.ds(pl.multiple_of(cols[k] * BS, BS), BS),
                    ],
                    tiles.at[f, k, pl.ds(i * BS, BS)],
                    sem.at[f, k, i],
                ).start()
    sub = BS // (nz * nx)
    for f in range(fronts):
        total = None
        for k in range(nc):
            for i in range(nr):
                pltpu.make_async_copy(
                    inv.at[pl.ds(0, BS), pl.ds(0, BS)],
                    tiles.at[f, k, pl.ds(i * BS, BS)],
                    sem.at[f, k, i],
                ).wait()
            term = dot3(split(tiles[f, k]), split(w[owners[f][k], f]))
            total = term if total is None else total + term
        for i in range(nr):
            for s in range(nx):
                for z in range(nz):
                    at = i * BS + (s * nz + z) * sub
                    out[f, s, i, z] = total[at : at + sub]


MESH = pl.DeviceIdType.MESH


def greet(peers):
    barrier = pltpu.get_barrier_semaphore()
    for peer in peers:
        pl.semaphore_signal(barrier, inc=1, device_id=peer, device_id_type=MESH)
    pl.semaphore_wait(barrier, len(peers))


class Mail:
    def __init__(self, send_sem, recv_sem):
        self.send_sem, self.recv_sem = send_sem, recv_sem
        self.sent = []

    def send(self, src, dst, peer):
        at = len(self.sent)
        copy = pltpu.make_async_remote_copy(
            src_ref=src,
            dst_ref=dst,
            send_sem=self.send_sem.at[at],
            recv_sem=self.recv_sem.at[at],
            device_id=peer,
            device_id_type=MESH,
        )
        copy.start()
        self.sent.append(copy)
        return copy

    def close(self):
        for copy in self.sent:
            copy.wait_send()


def gather_kernel(dims, fb, panels, out, send_sem, recv_sem):
    fronts, n_row, cg, cuts = dims
    r = lax.axis_index("row")
    c = lax.axis_index("col")
    core, y, ny = lax.rem(r, 2), r // 2, n_row // 2
    partner = r + 1 - 2 * core
    lines = [lax.rem(y + d, ny) * 2 + core for d in range(1, ny)]
    greet([(partner, c)] + [(line, c) for line in lines])
    per_owner = panels.shape[1]
    mail = Mail(send_sem, recv_sem)
    height = BS // cuts
    arriving, relayed = [], []
    for f in range(fronts):
        at = jnp.int32(0)
        found = jnp.int32(0)
        for j in range(per_owner):
            hit = (fb[f, r * per_owner + j] // cg) == c
            at = jnp.where(hit, j, at)
            found = jnp.where(hit, 1, found)
        out[r, f] = jnp.where(found == 1, panels[f, at], 0.0)
        for h in range(cuts):
            rows = pl.ds(h * height, height)
            for d, line in enumerate(lines, 1):
                piece = out.at[r, f, rows]
                came = lax.rem(y + ny - d, ny) * 2 + core
                arriving.append((mail.send(piece, piece, (line, c)), came, f, rows))
        mine = out.at[r, f]
        relayed.append(mail.send(mine, mine, (partner, c)))
    for copy, came, f, rows in arriving:
        copy.wait_recv()
        piece = out.at[came, f, rows]
        relayed.append(mail.send(piece, piece, (partner, c)))
    for copy in relayed:
        copy.wait_recv()
    mail.close()


def copies_of(dims):
    fronts, kb, nr, nc, rg, cg, nz, nx = dims
    n_row, n_col = kb // nr, kb // nc
    total = nr * (nx - 1) + nr * (nz - 1) + (n_row - 1) + (nz - 1)
    return fronts * (total + 2 * (1 + n_row // 2 - 1 + n_col - 1))


def sum_kernel(dims, fb, partial, w, border, acc, xbuf, xs, zbuf, zs, slots, rbuf, qs, cbuf, ybuf, lbuf, red, send_sem, recv_sem):
    fronts, kb, nr, nc, rg, cg, nz, nx = dims
    n_row, n_col = kb // nr, kb // nc
    per_owner = kb // n_row
    r = lax.axis_index("row")
    c = lax.axis_index("col")
    s, z = lax.rem(c, nx), c // nx
    core, y, ny = lax.rem(r, 2), r // 2, n_row // 2
    partner = r + 1 - 2 * core
    other = 1 - core
    cols = [lax.rem(c + d, n_col) for d in range(1, n_col)]
    rows = [lax.rem(r + d, n_row) for d in range(1, n_row)]
    greet([(r, col) for col in cols] + [(row, c) for row in rows])
    mail = Mail(send_sem, recv_sem)
    share = border.shape[1] * border.shape[2]
    part = acc.shape[4]
    sub = zs.shape[2]

    along_x = {}
    for f in range(fronts):
        for n in range(nr):
            for d in range(1, nx):
                to = lax.rem(s + d, nx)
                along_x[f, n, d] = mail.send(
                    partial.at[f, to, n], xbuf.at[f, n, d - 1], (r, z * nx + to)
                )

    along_z = {}

    def x_sum(f, n):
        for d in range(1, nx):
            along_x[f, n, d].wait_recv()
        total = partial[f, s, n]
        for d in range(1, nx):
            total = total + xbuf[f, n, d - 1]
        xs[f, n] = total
        for d in range(1, nz):
            to = lax.rem(z + d, nz)
            along_z[f, n, d] = mail.send(
                xs.at[f, n, to], zbuf.at[f, n, d - 1], (r, to * nx + s)
            )

    def z_sum(f, n):
        for d in range(1, nz):
            along_z[f, n, d].wait_recv()
        total = xs[f, n, z]
        for d in range(1, nz):
            total = total + zbuf[f, n, d - 1]
        zs[f, n] = total

    along_row = {}

    def row_send(f):
        if nr == n_row:
            source = zs
        else:
            source = slots
            n = jnp.int32(0)
            for row in range(n_row):
                named = jnp.int32(0)
                for j in range(per_owner):
                    named = jnp.where((fb[f, row * per_owner + j] // rg) == r, 1, named)
                slots[f, row] = jnp.where(named == 1, zs[f, jnp.minimum(n, nr - 1)], 0.0)
                n = n + named
        rbuf[f][r] = source[f, r]
        for d in range(1, n_row):
            to = rows[d - 1]
            along_row[f, d] = mail.send(source.at[f, to], rbuf[f].at[r], (to, c))

    along_owner = {}

    def owner_send(f):
        for d in range(1, n_row):
            along_row[f, d].wait_recv()
        for q in range(nz):
            qs[f, q] = rbuf[f][fb[f, r * per_owner + q] // rg]
        border[f, z] = qs[f, z]
        for d in range(1, nz):
            to = lax.rem(z + d, nz)
            along_owner[f, d] = mail.send(qs.at[f, to], border.at[f, z], (r, to * nx + s))

    to_core = {}

    def product(f):
        for d in range(1, nz):
            along_owner[f, d].wait_recv()
        wh, wl = split(w[f, pl.ds(pl.multiple_of(c * share, share), share)])
        ph, plo = split(jnp.concatenate([border[f, q] for q in range(nz)], axis=0))
        dot = functools.partial(
            lax.dot_general,
            dimension_numbers=(((0,), (0,)), ((), ())),
            preferred_element_type=jnp.float32,
        )
        total = dot(wh, ph) + (dot(wh, plo) + dot(wl, ph))
        for a in range(2):
            for b in range(ny):
                for e in range(n_col):
                    at = ((a * ny + b) * n_col + e) * part
                    red[f, a, b, e] = total[at : at + part]
        to_core[f] = mail.send(red.at[f, other], cbuf.at[f], (partner, c))

    to_y = {}

    def core_sum(f):
        to_core[f].wait_recv()
        red[f, core] = red[f, core] + cbuf[f]
        for d in range(1, ny):
            to = lax.rem(y + d, ny)
            to_y[f, d] = mail.send(
                red.at[f, core, to], ybuf.at[f, d - 1], (to * 2 + core, c)
            )

    to_col = {}

    def y_sum(f):
        for d in range(1, ny):
            to_y[f, d].wait_recv()
        total = red[f, core, y]
        for d in range(1, ny):
            total = total + ybuf[f, d - 1]
        red[f, core, y] = total
        for d in range(1, n_col):
            to = cols[d - 1]
            to_col[f, d] = mail.send(red.at[f, core, y, to], lbuf.at[f, d - 1], (r, to))

    back_col = {}

    def col_sum(f):
        for d in range(1, n_col):
            to_col[f, d].wait_recv()
        total = red[f, core, y, c]
        for d in range(1, n_col):
            total = total + lbuf[f, d - 1]
        acc[f, core, y, c] = total
        mine = acc.at[f, core, y, c]
        for d in range(1, n_col):
            back_col[f, d] = mail.send(mine, mine, (r, cols[d - 1]))

    back_y = {}

    def y_back(f):
        for d in range(1, n_col):
            back_col[f, d].wait_recv()
        mine = acc.at[f, core, y]
        for d in range(1, ny):
            to = lax.rem(y + d, ny)
            back_y[f, d] = mail.send(mine, mine, (to * 2 + core, c))

    back_core = {}

    def core_back(f):
        for d in range(1, ny):
            back_y[f, d].wait_recv()
        mine = acc.at[f, core]
        back_core[f] = mail.send(mine, mine, (partner, c))

    def finish(f):
        back_core[f].wait_recv()

    tail = (row_send, owner_send, product, core_sum, y_sum, col_sum, y_back, core_back, finish)
    steps = []
    for f in range(fronts):
        heads = [functools.partial(x_sum, f, n) for n in range(nr)]
        mids = [functools.partial(z_sum, f, n) for n in range(nr)]
        ends = [functools.partial(step, f) for step in tail]
        steps.append(heads + mids + ends)
    for step in steps[0][:nr]:
        step()
    ahead = steps[0][nr:]
    for later in steps[1:]:
        for i, step in enumerate(later):
            step()
            count = 2 if i < 2 or i == 3 else 1
            for move in ahead[:count]:
                move()
            ahead = ahead[count:]
    for move in ahead:
        move()
    mail.close()


def body(inverse, front_blocks, panels, diag_terms, bounds):
    n_row = lax.axis_size("row")
    n_col = lax.axis_size("col")
    r = lax.axis_index("row")
    c = lax.axis_index("col")
    rows_loc, cols_loc = inverse.shape
    rg = rows_loc // BS
    cg = cols_loc // BS
    fronts, kb = front_blocks.shape
    width = panels.shape[2]
    per_owner = kb // n_row
    nr = kb // n_row
    nc = kb // n_col
    nz = per_owner
    nx = n_col // nz
    sub = BS // n_col
    share = nz * sub

    cuts = 2
    gdims = (fronts, n_row, cg, cuts)
    count = fronts * (cuts * 2 * (n_row // 2 - 1) + 1)
    vmem = pl.BlockSpec(memory_space=pltpu.VMEM)
    smem = pl.BlockSpec(memory_space=pltpu.SMEM)
    gathered = pl.pallas_call(
        functools.partial(gather_kernel, gdims),
        out_shape=jax.ShapeDtypeStruct((n_row, fronts, BS, width), jnp.float32),
        in_specs=[smem, vmem],
        out_specs=vmem,
        scratch_shapes=[pltpu.SemaphoreType.DMA((count,))] * 2,
        compiler_params=pltpu.CompilerParams(
            collective_id=0, has_side_effects=True, vmem_limit_bytes=24 << 20
        ),
    )(front_blocks, panels.reshape(fronts, per_owner, BS, width))

    dims = (fronts, kb, nr, nc, rg, cg, nz, nx)
    partial = pl.pallas_call(
        functools.partial(tile_kernel, dims),
        out_shape=jax.ShapeDtypeStruct((fronts, nx, nr, nz, sub, width), jnp.float32),
        in_specs=[
            pl.BlockSpec(memory_space=pltpu.SMEM),
            pl.BlockSpec(memory_space=pl.ANY),
            pl.BlockSpec(memory_space=pltpu.VMEM),
        ],
        out_specs=pl.BlockSpec(memory_space=pltpu.VMEM),
        scratch_shapes=[
            pltpu.VMEM((fronts, nc, nr * BS, BS), jnp.float32),
            pltpu.SemaphoreType.DMA((fronts, nc, nr)),
        ],
        compiler_params=pltpu.CompilerParams(vmem_limit_bytes=40 << 20),
    )(front_blocks, inverse, gathered)

    ny = n_row // 2
    part = width // (n_row * n_col)
    count = copies_of(dims)
    f32 = jnp.float32
    border, acc = pl.pallas_call(
        functools.partial(sum_kernel, dims),
        out_shape=(
            jax.ShapeDtypeStruct((fronts, nz, sub, width), f32),
            jax.ShapeDtypeStruct((fronts, 2, ny, n_col, part, width), f32),
        ),
        in_specs=[smem, vmem, vmem],
        out_specs=(vmem, vmem),
        scratch_shapes=[
            pltpu.VMEM((fronts, nr, nx - 1, nz, sub, width), f32),
            pltpu.VMEM((fronts, nr, nz, sub, width), f32),
            pltpu.VMEM((fronts, nr, nz - 1, sub, width), f32),
            pltpu.VMEM((fronts, nr, sub, width), f32),
            pltpu.VMEM((fronts, n_row, sub, width), f32),
            [pltpu.VMEM((n_row, sub, width), f32)] * fronts,
            pltpu.VMEM((fronts, nz, sub, width), f32),
            pltpu.VMEM((fronts, ny, n_col, part, width), f32),
            pltpu.VMEM((fronts, ny - 1, n_col, part, width), f32),
            pltpu.VMEM((fronts, n_col - 1, part, width), f32),
            pltpu.VMEM((fronts, 2, ny, n_col, part, width), f32),
            pltpu.SemaphoreType.DMA((count,)),
            pltpu.SemaphoreType.DMA((count,)),
        ],
        compiler_params=pltpu.CompilerParams(
            collective_id=1, has_side_effects=True, vmem_limit_bytes=40 << 20
        ),
    )(front_blocks, partial, panels)
    product = border.reshape(fronts, share, width)
    summed = acc.reshape(fronts, width, width)
    ends = jnp.cumsum(bounds, axis=1)
    columns = jnp.arange(width, dtype=jnp.int32)
    ids = jnp.sum((columns[None, :, None] >= ends[:, None, :]).astype(jnp.int32), axis=2)
    same = (ids[:, :, None] == ids[:, None, :]).astype(jnp.float32)
    return (-product, same * (diag_terms + summed))


def solution(mesh):
    placed = (P("row", "col"), P(), P(None, "row", None), P(), P())
    return jax.shard_map(
        body,
        mesh=mesh,
        in_specs=placed,
        out_specs=(P(None, ("row", "col"), None), P()),
        check_vma=False,
    )
```
